32 devices in a mesh: dp: 16 (over z, y, core), fsdp: 2 (over x).
Axes of the slice: x: 2, y: 2, z: 4, core: 2. Of those that a mesh axis runs over, the one named last changes fastest.
Arguments:
- tokens: bfloat16 [256, 2, 64, 768], P(('dp', 'fsdp')), may hold values from -6 to 6
- lengths: int32 [256, 2], P(('dp', 'fsdp')), may hold values from 16 to 64
- pair_language: int32 [256], P(('dp', 'fsdp')), may hold values from 0 to 108
- query_weight: bfloat16 [768, 768], P('fsdp'), may hold values from -0.21875 to 0.21875
- key_weight: bfloat16 [768, 768], P('fsdp'), may hold values from -0.21875 to 0.21875
- value_weight: bfloat16 [768, 768], P('fsdp'), may hold values from -0.21875 to 0.21875
- output_weight: bfloat16 [768, 768], P('fsdp'), may hold values from -0.625 to 0.625
- query_bias: bfloat16 [768], P('fsdp'), may hold values from -1.75 to 1.75
- value_bias: bfloat16 [768], P('fsdp'), may hold values from -1.75 to 1.75
- output_bias: bfloat16 [768], P('fsdp'), may hold values from -1.75 to 1.75
- first_gain: bfloat16 [768], P('fsdp'), may hold values from 0.5 to 1.5
- first_shift: bfloat16 [768], P('fsdp'), may hold values from -1.75 to 1.75
- inner_weight: bfloat16 [768, 3072], P(None, 'fsdp'), may hold values from -0.21875 to 0.21875
- inner_bias: bfloat16 [3072], P('fsdp'), may hold values from -3 to 3
- outer_weight: bfloat16 [3072, 768], P('fsdp'), may hold values from -0.109375 to 0.109375
- outer_bias: bfloat16 [768], P('fsdp'), may hold values from -1.75 to 1.75
- second_gain: bfloat16 [768], P('fsdp'), may hold values from 0.5 to 1.5
- second_shift: bfloat16 [768], P('fsdp'), may hold values from -0.625 to 0.625
Outputs:
- activations: bfloat16 [256, 2, 64, 768], P(('dp', 'fsdp'))
- input_grad: float32 [256, 2, 64, 768], P(('dp', 'fsdp'))
- query_weight_grad: float32 [768, 768], P('fsdp')
- key_weight_grad: float32 [768, 768], P('fsdp')
- value_weight_grad: float32 [768, 768], P('fsdp')
- output_weight_grad: float32 [768, 768], P('fsdp')
- query_bias_grad: float32 [768], P('fsdp')
- value_bias_grad: float32 [768], P('fsdp')
- output_bias_grad: float32 [768], P('fsdp')
- first_gain_grad: float32 [768], P('fsdp')
- first_shift_grad: float32 [768], P('fsdp')
- inner_weight_grad: float32 [768, 3072], P(None, 'fsdp')
- inner_bias_grad: float32 [3072], P('fsdp')
- outer_weight_grad: float32 [3072, 768], P('fsdp')
- outer_bias_grad: float32 [768], P('fsdp')
- second_gain_grad: float32 [768], P('fsdp')
- second_shift_grad: float32 [768], P('fsdp')
The draws below stay inside these ranges and needn't reach their ends.
All inputs are finite; a program needn't handle non-finite values.
Results may differ from the reference program's by a relative error of at most 0.02.
Values may be sent and summed in bfloat16 or wider, within the bound.
No kernel may reach another device: no remote copies, remote signals or barrier semaphores. Data moves between devices by JAX's collectives and lax.ppermute only.
A program may use at most 256 MiB of HBM per device.

```python
import math
from functools import partial
import jax
import jax.numpy as jnp
import numpy as np
from jax import lax

D = 768
HEADS = 12
HEAD = 64
FF = 3072
SEQ = 64
PAIRS_DEV = 8
MB = 2
LANGS = 109
PAIRS = 256
N_DP = 16
N_FSDP = 2


def plant(entries, own_key, least, high):
    shape = entries.shape
    spot = [jax.random.randint(jax.random.fold_in(own_key, axis), (), 0, shape[axis]) for axis in range(len(shape))]
    entries = entries.at[tuple(spot)].set(least)
    longest = shape.index(max(shape))
    spot[longest] = (spot[longest] + 1) % shape[longest]
    return entries.at[tuple(spot)].set(high)


def level_of(own_key, extent, split, low, largest):
    factor_of = 1.0
    for dim, blocks in split:
        draws = jax.random.uniform(jax.random.fold_in(jax.random.fold_in(own_key, 6), dim), (blocks,), jnp.float32, low / len(split), largest / len(split))
        factor_of = factor_of * jnp.repeat(jnp.exp(draws), extent[dim] // blocks).reshape((-1,) + (1,) * (len(extent) - 1 - dim))
    return factor_of


def rank_bounds(amount, skew):
    weights = [(1 << 20) // math.isqrt(grade ** skew) + 1 for grade in range(1, amount + 1)]
    scale = 1 + sum(weights) // (1 << 30)
    return np.cumsum(np.array([max(1, weight // scale) for weight in weights]))


def ranked(rng, shape, number_of, skew):
    table = rank_bounds(number_of, skew)
    lot = jax.random.randint(jax.random.fold_in(rng, 1), shape, 0, int(table[number_of - 1]))
    standing = jnp.searchsorted(jnp.asarray(table, jnp.int32), lot, side="right")
    return jax.random.permutation(jax.random.fold_in(rng, 2), number_of)[standing].astype(jnp.int32)


def bell_draw(key, shape, width, reach, split=(), held_as=jnp.bfloat16):
    array = width * jax.random.normal(key, shape, jnp.float32)
    if split:
        array = array * level_of(key, shape, split, -0.22, 0.18)
    return jnp.clip(array, -reach, reach).astype(held_as)


def setup_inputs(seed: int = 0) -> dict:
    key_list = jax.random.split(jax.random.key(seed), 19)
    return {
        "tokens": bell_draw(key_list[0], (PAIRS, 2, SEQ, D), 1.0, 6.0, ((0, 32),)),
        "lengths": plant(jax.random.randint(key_list[1], (PAIRS, 2), SEQ // 4, SEQ + 1), jax.random.fold_in(key_list[1], 1), SEQ // 4, SEQ).astype(jnp.int32),
        "pair_language": plant(ranked(key_list[2], (PAIRS,), LANGS, 2), jax.random.fold_in(key_list[2], 3), 0, LANGS - 1).astype(jnp.int32),
        "query_weight": bell_draw(key_list[3], (D, D), D ** -0.5, 0.21875, ((0, 2),)),
        "key_weight": bell_draw(key_list[4], (D, D), D ** -0.5, 0.21875, ((0, 2),)),
        "value_weight": bell_draw(key_list[5], (D, D), D ** -0.5, 0.21875, ((0, 2),)),
        "output_weight": bell_draw(key_list[6], (D, D), (D // 8) ** -0.5, 0.625, ((0, 2),)),
        "query_bias": bell_draw(key_list[7], (D,), 0.3, 1.75, ((0, 2),)),
        "value_bias": bell_draw(key_list[8], (D,), 0.3, 1.75, ((0, 2),)),
        "output_bias": bell_draw(key_list[9], (D,), 0.3, 1.75, ((0, 2),)),
        "first_gain": jnp.clip(1.0 + 0.1 * jax.random.normal(key_list[10], (D,), jnp.float32), 0.5, 1.5).astype(jnp.bfloat16),
        "first_shift": bell_draw(key_list[11], (D,), 0.3, 1.75, ((0, 2),)),
        "inner_weight": bell_draw(key_list[12], (D, FF), D ** -0.5, 0.21875, ((1, 2),)),
        "inner_bias": bell_draw(key_list[13], (FF,), 0.5, 3.0, ((0, 2),)),
        "outer_weight": bell_draw(key_list[14], (FF, D), FF ** -0.5, 0.109375, ((0, 2),)),
        "outer_bias": bell_draw(key_list[15], (D,), 0.3, 1.75, ((0, 2),)),
        "second_gain": jnp.clip(1.0 + 0.1 * jax.random.normal(key_list[16], (D,), jnp.float32), 0.5, 1.5).astype(jnp.bfloat16),
        "second_shift": bell_draw(key_list[17], (D,), 0.1, 0.625, ((0, 2),)),
    }


eps_norm = 1e-06
score_scale = 50.0
margin = 0.3
loss_scale = 64.0
neg_fill = -1e+30
highest = lax.Precision.HIGHEST

@jax.custom_vjp
def low(v):
    return lax.optimization_barrier(v.astype(jnp.bfloat16)).astype(jnp.float32)

@jax.custom_vjp
def low_back(v):
    return v

def low_keep(v):
    return (low(v), None)

def low_pass(kept, grad):
    return (grad,)

def back_keep(v):
    return (v, None)

def back_low(kept, grad):
    return (low(grad),)
low.defvjp(low_keep, low_pass)
low_back.defvjp(back_keep, back_low)

def both_round(value):
    return low_back(low(value))

def layer_norm(resid, gain, shift):
    centre = resid - lax.optimization_barrier(jnp.mean(resid, axis=-1, keepdims=True))
    spread = lax.optimization_barrier(jnp.mean(centre * centre, axis=-1, keepdims=True))
    return centre * lax.rsqrt(spread + eps_norm) * gain + shift

def normalize(pooled):
    scale = lax.rsqrt(lax.optimization_barrier(jnp.mean(pooled * pooled, axis=-1, keepdims=True)) + eps_norm)
    return pooled * scale / math.sqrt(pooled.shape[-1])

def encode(params, block):
    query_weight, key_weight, value_weight, output_weight, query_bias, value_bias, output_bias, first_gain, first_shift, inner_weight, inner_bias, outer_weight, outer_bias, second_gain, second_shift = params
    sentences_in, lens = block
    count = sentences_in.shape[0]
    flat = sentences_in.reshape(count * SEQ, D)
    split_shape = (count, SEQ, HEADS, HEAD)
    query = both_round(jnp.dot(flat, query_weight, precision=highest) + query_bias)
    keys = both_round(jnp.dot(flat, key_weight, precision=highest))
    values = both_round(jnp.dot(flat, value_weight, precision=highest) + value_bias)
    scores = jnp.einsum('nqhd,nkhd->nhqk', query.reshape(split_shape), keys.reshape(split_shape), precision=highest) * HEAD ** (-0.5)
    scores = low_back(scores)
    key_mask = jnp.arange(SEQ)[None, :] < lens[:, None]
    scores = jnp.where(key_mask[:, None, None, :], scores, neg_fill)
    probs = low(jax.nn.softmax(scores, axis=-1))
    attended = jnp.einsum('nhqk,nkhd->nqhd', probs, values.reshape(split_shape), precision=highest)
    attended = both_round(attended.reshape(count * SEQ, D))
    resid_one = flat + low_back(jnp.dot(attended, output_weight, precision=highest) + output_bias)
    hidden_one = layer_norm(resid_one, first_gain, first_shift)
    inner = low_back(jnp.dot(low(hidden_one), inner_weight, precision=highest) + inner_bias)
    active = low(jax.nn.gelu(inner, approximate=False))
    resid_two = hidden_one + low_back(jnp.dot(active, outer_weight, precision=highest) + outer_bias)
    final = layer_norm(resid_two, second_gain, second_shift)
    return final.reshape(count, SEQ, D)

def pair_scores_loss(source, target, langs):
    count = source.shape[0]
    identity = jnp.arange(count)[:, None] == jnp.arange(count)[None, :]
    scores = score_scale * jnp.dot(source, target.T, precision=highest) - score_scale * margin * identity
    allowed = langs[:, None] == langs[None, :]
    masked = jnp.where(allowed, scores, neg_fill)
    diagonal = lax.optimization_barrier(jnp.sum(jnp.where(identity, scores, 0.0), axis=1))
    row_part = jnp.sum(jax.nn.logsumexp(masked, axis=1) - diagonal)
    col_part = jnp.sum(jax.nn.logsumexp(masked, axis=0) - diagonal)
    return loss_scale * (row_part + col_part)

def total_loss(params, tokens_f, lengths, langs):
    devices = N_DP * N_FSDP
    per_micro = PAIRS_DEV // MB
    group = 32
    blocked = tokens_f.reshape(devices, MB, per_micro, 2, SEQ, D)
    lens_blocked = lengths.reshape(devices, MB, per_micro, 2)
    lang_blocked = langs.reshape(devices, MB, per_micro)
    loss = jnp.float32(0.0)
    finals = []
    for micro in range(MB):
        sentences_in = blocked[:, micro].reshape(-1, group, SEQ, D)
        lens = lens_blocked[:, micro].reshape(-1, group)
        final = lax.map(jax.checkpoint(partial(encode, params)), (sentences_in, lens))
        final = final.reshape(devices * per_micro, 2, SEQ, D)
        lens_pairs = lens_blocked[:, micro].reshape(devices * per_micro, 2)
        mask = jnp.arange(SEQ)[None, None, :] < lens_pairs[:, :, None]
        pooled = lax.optimization_barrier(jnp.sum(jnp.where(mask[..., None], final, 0.0), axis=2)) / lens_pairs[..., None].astype(jnp.float32)
        unit = normalize(pooled)
        loss = loss + pair_scores_loss(unit[:, 0], unit[:, 1], lang_blocked[:, micro].reshape(-1))
        finals.append(final.reshape(devices, per_micro, 2, SEQ, D))
    acts = jnp.stack(finals, axis=1).reshape(devices * PAIRS_DEV, 2, SEQ, D)
    return (loss, acts)

def reference(tokens, lengths, pair_language, query_weight, key_weight, value_weight, output_weight, query_bias, value_bias, output_bias, first_gain, first_shift, inner_weight, inner_bias, outer_weight, outer_bias, second_gain, second_shift):
    params = tuple((item.astype(jnp.float32) for item in (query_weight, key_weight, value_weight, output_weight, query_bias, value_bias, output_bias, first_gain, first_shift, inner_weight, inner_bias, outer_weight, outer_bias, second_gain, second_shift)))
    tokens_f = tokens.astype(jnp.float32)

    def objective(weights, inputs):
        return total_loss(weights, inputs, lengths, pair_language)
    loss_value, pullback, acts = jax.vjp(objective, params, tokens_f, has_aux=True)
    grads, token_grad = pullback(jnp.ones_like(loss_value))
    return (acts.astype(jnp.bfloat16), token_grad, grads[0], grads[1], grads[2], grads[3], grads[4], grads[5], grads[6], grads[7], grads[8], grads[9], grads[10], grads[11], grads[12], grads[13], grads[14])
```

```python
import math

import jax
import jax.numpy as jnp
from jax import lax
from jax.experimental import pallas as pl
from jax.experimental.pallas import tpu as pltpu
from jax.sharding import PartitionSpec as P

HEADS = 12
MB = 2
QUAD = 4
GROUP = 4

eps_norm = 1e-06
score_scale = 50.0
margin = 0.3
loss_scale = 64.0
neg_fill = -1e30
highest = lax.Precision.HIGHEST
bf16 = jnp.bfloat16
f32 = jnp.float32


FULL = pl.BlockSpec(memory_space=pltpu.VMEM)
SCALARS = pl.BlockSpec(memory_space=pltpu.SMEM)


def mm(left, right):
    return jnp.dot(left, right, preferred_element_type=f32)


def mm_cols(left, right):
    return lax.dot_general(left, right, (((1,), (1,)), ((), ())), preferred_element_type=f32)


def mm_rows(left, right):
    return lax.dot_general(left, right, (((0,), (0,)), ((), ())), preferred_element_type=f32)


def row_mean(value):
    return jnp.mean(value, axis=-1, keepdims=True)


def whole(shape):
    return pl.BlockSpec(shape, lambda i: (0,) * len(shape), pipeline_mode=pl.Buffered(1))


def rows_of(shape):
    return pl.BlockSpec(shape, lambda i: (i,) + (0,) * (len(shape) - 1))


def params(limit_mib):
    return pltpu.CompilerParams(
        dimension_semantics=("arbitrary",), vmem_limit_bytes=limit_mib * 1024 * 1024
    )


def lane_group(shape, head):
    lane = lax.broadcasted_iota(jnp.int32, shape, len(shape) - 1)
    return (lane >= head * head_of(shape)) & (lane < (head + 1) * head_of(shape))


def head_of(shape):
    return shape[-1] // QUAD


def spread_heads(block):
    zero = jnp.zeros_like(block)
    return jnp.concatenate(
        [jnp.where(lane_group(block.shape, head), block, zero) for head in range(QUAD)], axis=0
    )


def pick_heads(stack, seq):
    out = stack[0:seq]
    for head in range(1, QUAD):
        out = jnp.where(
            lane_group(out.shape, head), stack[head * seq : (head + 1) * seq], out
        )
    return out


def seg_reduce(value, op, fill, seg):
    outs = []
    pair = 2 * seg
    for start in range(0, value.shape[-1], pair):
        part = value[:, start : start + pair]
        lane = lax.broadcasted_iota(jnp.int32, part.shape, 1)
        first = op(jnp.where(lane < seg, part, fill), axis=-1, keepdims=True)
        second = op(jnp.where(lane < seg, fill, part), axis=-1, keepdims=True)
        outs.append(jnp.where(lane < seg, first, second))
    return jnp.concatenate(outs, axis=-1)


def probs_of(query, spread_keys, length, factor, seq):
    scores = mm_cols(query, spread_keys) * factor
    lane = lax.broadcasted_iota(jnp.int32, scores.shape, 1)
    scores = jnp.where(lane % seq < length, scores, neg_fill)
    top = seg_reduce(scores, jnp.max, neg_fill, seq)
    exps = jnp.exp(scores - top)
    return exps / seg_reduce(exps, jnp.sum, 0.0, seq)


SLOTS = 4


def fill_square(full_ref, own_ref, where, near, far, offset):
    half = own_ref.shape[0]
    full_ref[pl.ds(pl.multiple_of(where[0] * half, 128), half), :] = own_ref[...]
    fill_other(full_ref, where, near, far, offset, half // (2 * SLOTS), (1 - where[0]) * half)


def fill_other(ref, where, near, far, offset, rows, base=0, cols=slice(None)):
    size = near.shape[0] // SLOTS
    for slot in range(2 * SLOTS):
        source = near if slot < SLOTS else far
        at = (slot % SLOTS) * size + offset
        spot = pl.multiple_of(base + where[1 + slot] * rows, 16)
        ref[pl.ds(spot, rows), cols] = source[at : at + rows, :]


def attention_forward(seq, factor, first, spare):
    def kernel(lens, where, tokens, vec, wq, wk, wv, near, far, *rest):
        q_ref, k_ref, v_ref, a_ref, p_ref, mark, fq, fk, fv = rest[spare:]
        step = pl.program_id(0)

        @pl.when(step == 0)
        def _():
            rows = wq.shape[0] // (2 * SLOTS)
            for slot, (full, own) in enumerate(((fq, wq), (fk, wk), (fv, wv))):
                fill_square(full, own, where, near, far, slot * rows)
            mark[...] = jnp.zeros_like(mark)

        block = tokens[...]
        query = (mm(block, fq[...]) + vec[0:1, :]).astype(bf16)
        keys = mm(block, fk[...]).astype(bf16)
        values = (mm(block, fv[...]) + vec[1:2, :]).astype(bf16)
        q_ref[...] = query
        k_ref[...] = keys
        v_ref[...] = values
        wide = block.shape[1] // (HEADS // QUAD)
        for item in range(GROUP):
            length = lens[(first + step) * GROUP + item]
            rs = slice(item * seq, (item + 1) * seq)
            for quad in range(HEADS // QUAD):
                cs = slice(quad * wide, (quad + 1) * wide)
                probs = probs_of(query[rs, cs], spread_heads(keys[rs, cs]), length, factor, seq)
                p_ref[rs, cs] = probs
                a_ref[rs, cs] = mm(probs.astype(bf16), spread_heads(values[rs, cs])).astype(bf16)

    return kernel


def fill_feed(where, own_o, near, far, fo, fi, fu):
    width = own_o.shape[1]
    at = own_o.shape[0] // (2 * SLOTS)
    if fo is not None:
        fill_square(fo, own_o, where, near, far, 0)
    deep = fi.shape[0] // (2 * SLOTS)
    for col in range(0, fi.shape[1], width):
        fill_other(fi, where, near, far, at, deep, 0, slice(col, col + width))
        at += deep
    fill_other(fu, where, near, far, at, fu.shape[0] // (2 * SLOTS))


def feed_forward(seq, block_cols):
    def kernel(
        lens, where, langs, tokens, attended, vec, bias, wo, wi, wu, near, far,
        xhat1_ref, s1_ref, h1_ref, g_ref, gp_ref, xhat2_ref, s2_ref, act_ref, pool_ref, pay_ref,
        fo, fi, fu,
    ):
        step = pl.program_id(0)

        @pl.when(step == 0)
        def _():
            fill_feed(where, wo, near, far, fo, fi, fu)

        resid = tokens[...].astype(f32) + mm(attended[...], fo[...]) + vec[2:3, :]
        centre = resid - row_mean(resid)
        s1 = lax.rsqrt(row_mean(centre * centre) + eps_norm)
        xhat1 = centre * s1
        hidden = xhat1 * vec[3:4, :] + vec[4:5, :]
        low = hidden.astype(bf16)
        xhat1_ref[...] = xhat1
        s1_ref[...] = jnp.broadcast_to(s1, s1_ref.shape)
        h1_ref[...] = low
        own = wi.shape[1]
        total = hidden + vec[5:6, :]
        for start in range(0, 2 * own, block_cols):
            cs = slice(start, start + block_cols)
            if start < own:
                w_in, w_out = wi[:, cs], wu[cs, :]
            else:
                os_ = slice(start - own, start - own + block_cols)
                w_in, w_out = fi[:, os_], fu[os_, :]
            inner = mm(low, w_in) + bias[0:1, cs]
            cdf = 0.5 * (1.0 + lax.erf(inner * (1.0 / math.sqrt(2.0))))
            active = (inner * cdf).astype(bf16)
            slope = cdf + inner * jnp.exp(-0.5 * inner * inner) * (1.0 / math.sqrt(2.0 * math.pi))
            g_ref[:, cs] = active
            gp_ref[:, cs] = slope.astype(bf16)
            total = total + mm(active, w_out)
        centre = total - row_mean(total)
        s2 = lax.rsqrt(row_mean(centre * centre) + eps_norm)
        xhat2 = centre * s2
        final = xhat2 * vec[6:7, :] + vec[7:8, :]
        xhat2_ref[...] = xhat2
        s2_ref[...] = jnp.broadcast_to(s2, s2_ref.shape)
        act_ref[...] = final.astype(bf16)
        width = final.shape[1]
        pairs = pool_ref.shape[0] // 2
        for item in range(GROUP):
            length = lens[step * GROUP + item]
            part = final[item * seq : (item + 1) * seq]
            row = lax.broadcasted_iota(jnp.int32, part.shape, 0)
            pooled = jnp.sum(jnp.where(row < length, part, 0.0), axis=0, keepdims=True)
            pooled = pooled / jnp.full((1, 1), length, jnp.int32).astype(f32)
            unit = pooled * lax.rsqrt(row_mean(pooled * pooled) + eps_norm) / math.sqrt(width)
            pair = step * (GROUP // 2) + item // 2
            spot = (item % 2) * pairs + pair
            lang = jnp.full((1, 128), langs[pair], jnp.int32).astype(f32)
            for ref, value in (
                (pool_ref, pooled), (pay_ref, jnp.concatenate([unit, lang], axis=1))
            ):
                line = lax.broadcasted_iota(jnp.int32, ref.shape, 0)
                ref[...] = jnp.where(line == spot, value, ref[...])

    return kernel


def feed_backward(seq, block_cols):
    def kernel(
        lens, where, dpool, vec, xhat2_ref, s2_ref, gp_ref, xhat1_ref, s1_ref, wo, wi, wu,
        near, far, dy_ref, dz_ref, dr1_ref, do_ref, sums_ref, inner_sums_ref, fi, fu,
    ):
        step = pl.program_id(0)

        @pl.when(step == 0)
        def _():
            fill_feed(where, wo, near, far, None, fi, fu)
            sums_ref[...] = jnp.zeros_like(sums_ref)
            inner_sums_ref[...] = jnp.zeros_like(inner_sums_ref)

        pairs = dpool.shape[0] // 2
        parts = []
        for item in range(GROUP):
            length = lens[step * GROUP + item]
            spot = (item % 2) * pairs + step * (GROUP // 2) + item // 2
            line = jnp.broadcast_to(dpool[pl.ds(spot, 1), :], (seq, dpool.shape[1]))
            row = lax.broadcasted_iota(jnp.int32, line.shape, 0)
            parts.append(jnp.where(row < length, line, 0.0))
        dout = jnp.concatenate(parts, axis=0)
        xhat2 = xhat2_ref[...]
        grad = dout * vec[6:7, :]
        dr2 = s2_ref[:, 0:1] * (grad - row_mean(grad) - xhat2 * row_mean(grad * xhat2))
        dy = dr2.astype(bf16)
        dy_ref[...] = dy
        dh1 = dr2
        own = wi.shape[1]
        for start in range(0, 2 * own, block_cols):
            cs = slice(start, start + block_cols)
            if start < own:
                w_in, w_out = wi[:, cs], wu[cs, :]
            else:
                os_ = slice(start - own, start - own + block_cols)
                w_in, w_out = fi[:, os_], fu[os_, :]
            dz = (mm_cols(dy, w_out) * gp_ref[:, cs].astype(f32)).astype(bf16)
            dz_ref[:, cs] = dz
            inner_sums_ref[0:1, cs] += jnp.sum(dz.astype(f32), axis=0, keepdims=True)
            dh1 = dh1 + mm_cols(dz, w_in)
        xhat1 = xhat1_ref[...]
        grad = dh1 * vec[3:4, :]
        dr1 = s1_ref[:, 0:1] * (grad - row_mean(grad) - xhat1 * row_mean(grad * xhat1))
        dr1_ref[...] = dr1
        do = dr1.astype(bf16)
        do_ref[...] = do
        for slot, value in enumerate(
            (do.astype(f32), dh1 * xhat1, dh1, dy.astype(f32), dout * xhat2, dout)
        ):
            sums_ref[slot : slot + 1, :] += jnp.sum(value, axis=0, keepdims=True)

    return kernel


def attention_backward(seq, factor, spare):
    def kernel(
        where, dr1_ref, q_ref, k_ref, v_ref, p_ref, wq, wk, wv, near, far, wo, near2, far2, *rest
    ):
        din_ref, dq_ref, dk_ref, dv_ref, sums_ref, fq, fk, fv, fo, da_ref = rest[spare:]
        step = pl.program_id(0)

        @pl.when(step == 0)
        def _():
            rows = wq.shape[0] // (2 * SLOTS)
            for slot, (full, own) in enumerate(((fq, wq), (fk, wk), (fv, wv))):
                fill_square(full, own, where, near, far, slot * rows)
            fill_square(fo, wo, where, near2, far2, 0)
            sums_ref[...] = jnp.zeros_like(sums_ref)

        dr1 = dr1_ref[...]
        da_ref[...] = mm_cols(dr1.astype(bf16), fo[...]).astype(bf16)
        wide = dr1.shape[1] // (HEADS // QUAD)
        for item in range(GROUP):
            rs = slice(item * seq, (item + 1) * seq)
            for quad in range(HEADS // QUAD):
                cs = slice(quad * wide, (quad + 1) * wide)
                query, da, probs = q_ref[rs, cs], da_ref[rs, cs], p_ref[rs, cs]
                dprobs = mm_cols(da, spread_heads(v_ref[rs, cs]))
                inner = seg_reduce(probs * dprobs, jnp.sum, 0.0, seq)
                dscores = (probs * (dprobs - inner)).astype(bf16)
                dq_ref[rs, cs] = (mm(dscores, spread_heads(k_ref[rs, cs])) * factor).astype(bf16)
                dk_ref[rs, cs] = (pick_heads(mm_rows(dscores, query), seq) * factor).astype(bf16)
                dv_ref[rs, cs] = pick_heads(mm_rows(probs.astype(bf16), da), seq).astype(bf16)
        dq, dk, dv = dq_ref[...], dk_ref[...], dv_ref[...]
        din_ref[...] = dr1 + mm_cols(dq, fq[...]) + mm_cols(dk, fk[...]) + mm_cols(dv, fv[...])
        for slot, value in enumerate((dq, dv)):
            sums_ref[slot : slot + 1, :] += jnp.sum(value.astype(f32), axis=0, keepdims=True)

    return kernel


def half_grad(left, right, lang_left, lang_right, own, per_pair):
    count = left.shape[0]
    scores = score_scale * lax.dot_general(
        left, right, (((1,), (1,)), ((), ())), precision=highest, preferred_element_type=f32
    )
    i = lax.broadcasted_iota(jnp.int32, scores.shape, 0)
    j = lax.broadcasted_iota(jnp.int32, scores.shape, 1)
    same = i == j
    scores = scores - jnp.where(same, score_scale * margin, 0.0)
    micro_i = (i % (MB * per_pair)) // per_pair
    micro_j = (j % (MB * per_pair)) // per_pair
    allowed = (lang_left == lang_right) & (micro_i == micro_j)
    scores = jnp.where(allowed, scores, neg_fill)
    head = scores[0:own]
    top = jnp.max(head, axis=1, keepdims=True)
    row_lse = top + jnp.log(jnp.sum(jnp.exp(head - top), axis=1, keepdims=True))
    top = jnp.max(scores, axis=0, keepdims=True)
    col_lse = top + jnp.log(jnp.sum(jnp.exp(scores - top), axis=0, keepdims=True))
    grad = jnp.exp(head - row_lse) + jnp.exp(head - col_lse) - jnp.where(same[0:own], 2.0, 0.0)
    return (
        jnp.dot(grad, right, precision=highest, preferred_element_type=f32)
        * (score_scale * loss_scale)
    )


def pool_grad(gathered_u, gathered_v, lang_col, lang_row, pooled, lens_col, own):
    per_pair = own // MB
    du = half_grad(gathered_u, gathered_v, lang_col, lang_row, own, per_pair)
    dv = half_grad(gathered_v, gathered_u, lang_col, lang_row, own, per_pair)
    grad = jnp.concatenate([du, dv], axis=0)
    scale = lax.rsqrt(row_mean(pooled * pooled) + eps_norm)
    grad = scale * (grad - pooled * (scale * scale) * row_mean(grad * pooled))
    return grad / math.sqrt(pooled.shape[1]) / lens_col


def loss_kernel(g_ref, pool_ref, lens_ref, out_ref):
    own = pool_ref.shape[0] // 2
    width = pool_ref.shape[1]
    count = g_ref.shape[0] * own
    source = g_ref[:, 0:own, 0:width].reshape(count, width)
    target = g_ref[:, own : 2 * own, 0:width].reshape(count, width)
    lang = g_ref[:, 0:own, width : width + 128].reshape(count, 128)
    out_ref[...] = pool_grad(
        source, target, lang[:, 0:1], lang.T[0:1, :], pool_ref[...], lens_ref[:, 0:1], own
    )


def swap(value, axis, size, mask):
    return lax.ppermute(value, axis, [(i, i ^ mask) for i in range(size)])


def cut(value, start, rows, axis=0):
    return lax.dynamic_slice_in_dim(value, start, rows, axis=axis)


def gather_units(payload, n_dp, n_fs, ring):
    out = payload[None]
    if not ring:
        every = lax.all_gather(payload, ("dp", "fsdp"), axis=0)
        me = lax.axis_index(("dp", "fsdp"))
        return jnp.roll(every, -me, axis=0)
    out = jnp.concatenate(
        [out] + [swap(out, "dp", n_dp, 4 * delta) for delta in range(1, n_dp // 4)], axis=0
    )
    from_x, from_y = swap(out, "fsdp", n_fs, 1), swap(out, "dp", n_dp, 2)
    middle = out.shape[0] // 2
    corner = [swap(from_x[:middle], "dp", n_dp, 2), swap(from_y[middle:], "fsdp", n_fs, 1)]
    out = jnp.concatenate([out, from_x, from_y] + corner, axis=0)
    return jnp.concatenate([out, swap(out, "dp", n_dp, 1)], axis=0)


class Chain:
    def __init__(self):
        self.last = None

    def __call__(self, value):
        if self.last is not None:
            value, _ = lax.optimization_barrier((value, self.last))
        self.last = value
        return value


class Pieces:
    def __init__(self, chain, n_dp, n_fs):
        self.chain, self.n_dp, self.n_fs = chain, n_dp, n_fs

    def over_x(self, piece):
        self.body = swap(self.chain(piece), "fsdp", self.n_fs, 1)

    def over_yz(self):
        body = self.chain(self.body)
        self.got = [body, swap(body, "dp", self.n_dp, 2), swap(body, "dp", self.n_dp, 4)]

    def over_corner(self):
        body, from_y, from_z = self.got
        middle = body.shape[0] // 16 * 8
        send_y, send_z = self.chain((from_y[:middle], from_z[middle:]))
        corner = [swap(send_y, "dp", self.n_dp, 4), swap(send_z, "dp", self.n_dp, 2)]
        self.near = jnp.concatenate(self.got + corner, axis=0)

    def over_core(self):
        self.near = self.chain(self.near)
        return self.near, swap(self.near, "dp", self.n_dp, 1)


def add(*values):
    total = values[0].astype(f32)
    for value in values[1:]:
        total = total + value.astype(f32)
    return total.astype(bf16)


class Reducer:
    def __init__(self, part, chain, n_dp, n_fs, dp_index):
        self.n_dp, self.n_fs, self.dp_index, self.chain = n_dp, n_fs, dp_index, chain
        core = dp_index & 1
        got = swap(chain(part(1 - core)), "dp", n_dp, 1)
        self.acc = add(part(core), got)

    def x(self):
        acc = self.acc = self.chain(self.acc)
        self.acc = add(acc[0:1], swap(acc[1:2], "fsdp", self.n_fs, 1))

    def y(self):
        acc = self.chain(self.acc)
        rows, mine = acc.shape[1] // 2, (self.dp_index >> 1) & 1
        got = swap(cut(acc, (1 - mine) * rows, rows, 1), "dp", self.n_dp, 2)
        self.acc = add(cut(acc, mine * rows, rows, 1), got)

    def z(self):
        acc, n_z = self.chain(self.acc), self.n_dp // 4
        rows, mine = acc.shape[1] // n_z, self.dp_index >> 2
        terms = [cut(acc, mine * rows, rows, 1)]
        for delta in range(1, n_z):
            send = cut(acc, (mine ^ delta) * rows, rows, 1)
            terms.append(swap(send, "dp", self.n_dp, 4 * delta))
        self.acc = add(*terms)

    def back_z(self):
        acc, n_z, mine = self.chain(self.acc)[0], self.n_dp // 4, self.dp_index >> 2
        got = [acc] + [swap(acc, "dp", self.n_dp, 4 * delta) for delta in range(1, n_z)]
        self.acc = jnp.concatenate(
            [lax.select_n(mine, *[got[j ^ m] for m in range(n_z)]) for j in range(n_z)], axis=0
        )

    def back_y(self):
        acc = self.chain(self.acc)
        got = swap(acc, "dp", self.n_dp, 2)
        ybit = (self.dp_index >> 1) & 1
        self.acc = jnp.where(
            ybit == 0, jnp.concatenate([acc, got], axis=0), jnp.concatenate([got, acc], axis=0)
        )

    def back_core(self):
        acc = self.chain(self.acc)
        got = swap(acc, "dp", self.n_dp, 1)
        core = self.dp_index & 1
        self.halves = jnp.where(core == 0, acc, got), jnp.where(core == 0, got, acc)


def step_body(n_dp, n_fs):
    ring = n_fs == 2 and n_dp == 16

    def body(
        tokens, lengths, pair_language, query_weight, key_weight, value_weight, output_weight,
        query_bias, value_bias, output_bias, first_gain, first_shift, inner_weight, inner_bias,
        outer_weight, outer_bias, second_gain, second_shift,
    ):
        pairs, _, seq, width = tokens.shape
        sentences = 2 * pairs
        total = sentences * seq
        half = width // 2
        small = (
            query_bias, value_bias, output_bias, first_gain, first_shift, outer_bias,
            second_gain, second_shift,
        )
        dp_index = lax.axis_index("dp")
        if ring:
            f = lax.axis_index("fsdp")
            spot = dp_index & 7
            own_q, own_k, own_v, own_o = query_weight, key_weight, value_weight, output_weight
            own_i, own_u = inner_weight, outer_weight
            rows, deep, tall = half // 8, width // 8, own_u.shape[0] // 8
            first = jnp.concatenate(
                [cut(w, spot * rows, rows) for w in (own_q, own_k, own_v)], axis=0
            )
            inner_rows = cut(own_i, spot * deep, deep)
            second = jnp.concatenate(
                [cut(own_o, spot * rows, rows)]
                + [inner_rows[:, c : c + width] for c in range(0, own_i.shape[1], width)]
                + [cut(own_u, spot * tall, tall)],
                axis=0,
            )
            chain = Chain()
            early, later = Pieces(chain, n_dp, n_fs), Pieces(chain, n_dp, n_fs)
            early.over_x(first)
            vectors = jnp.concatenate(small + (inner_bias,))
            other = swap(chain(vectors), "fsdp", n_fs, 1)
            later.over_x(second)
            early.over_yz()
            early.over_corner()
            near, far = early.over_core()
            later.over_yz()
            own8, other8 = [
                v[: len(small) * half].reshape(len(small), half) for v in (vectors, other)
            ]
            vec = jnp.where(
                f == 0,
                jnp.concatenate([own8, other8], axis=1),
                jnp.concatenate([other8, own8], axis=1),
            ).astype(f32)
            bias = jnp.concatenate([inner_bias, other[len(small) * half :]])[None].astype(f32)
        else:
            def gather(value, axis=0):
                return lax.all_gather(value, "fsdp", axis=axis, tiled=True)

            f, spot = jnp.int32(0), jnp.int32(0)
            full = [gather(w) for w in (query_weight, key_weight, value_weight, output_weight)]
            own_q, own_k, own_v, own_o = [w[:half] for w in full]
            wide_i, wide_u = gather(inner_weight, 1), gather(outer_weight)
            ff_half = wide_u.shape[0] // 2
            own_i, own_u = wide_i[:, :ff_half], wide_u[:ff_half]
            rows, deep, tall = half // 8, width // 8, ff_half // 8

            def square_part(w, n):
                return w[half + n * rows : half + (n + 1) * rows]

            def piece(n):
                lines = wide_i[n * deep : (n + 1) * deep, ff_half:]
                return jnp.concatenate(
                    [square_part(full[3], n)]
                    + [lines[:, c : c + width] for c in range(0, ff_half, width)]
                    + [wide_u[ff_half + n * tall : ff_half + (n + 1) * tall]],
                    axis=0,
                )

            near, far = [
                jnp.concatenate(
                    [square_part(w, n) for n in range(odd, 8, 2) for w in full[:3]], axis=0
                )
                for odd in (0, 1)
            ]
            near2, far2 = [
                jnp.concatenate([piece(n) for n in range(odd, 8, 2)], axis=0) for odd in (0, 1)
            ]
            vec = jnp.stack([gather(v) for v in small]).astype(f32)
            bias = gather(inner_bias)[None].astype(f32)

        lens = lengths.reshape(sentences)
        place = jnp.stack([f] + [spot ^ mask for mask in (0, 2, 4, 6, 1, 3, 5, 7)]).astype(jnp.int32)
        flat = tokens.reshape(total, width)
        factor = (width // HEADS) ** (-0.5)
        block = GROUP * seq
        steps = sentences // GROUP
        ff = 2 * own_u.shape[0]
        square = pltpu.VMEM((width, width), bf16)
        wide_rows = rows_of((block, width))

        def arr(cols, dtype, count=total):
            return jax.ShapeDtypeStruct((count, cols), dtype)

        def cost(flops, moved):
            return pl.CostEstimate(
                flops=int(flops), bytes_accessed=int(moved), transcendentals=0
            )

        mat = 2 * total * width * width
        any_space = pl.BlockSpec(memory_space=pl.ANY)
        parts = 2
        fewer = steps // parts

        def offset_rows(cols, n):
            return pl.BlockSpec((block, cols), lambda i: (i + n * fewer, 0))

        saved = ()
        for n in range(parts):
            operands = (lens, place, flat, vec, own_q, own_k, own_v, near, far)
            if ring:
                operands, _ = lax.optimization_barrier((operands, chain.last))
            *saved, mark = pl.pallas_call(
                attention_forward(seq, factor, n * fewer, len(saved)),
                grid=(fewer,),
                in_specs=[SCALARS, SCALARS, offset_rows(width, n)]
                + [whole(v.shape) for v in operands[3:]] + [any_space] * len(saved),
                out_specs=[offset_rows(width, n)] * 5 + [whole((8, 128))],
                out_shape=[arr(width, bf16)] * 4 + [arr(width, f32), arr(128, f32, 8)],
                scratch_shapes=[square] * 3,
                input_output_aliases={len(operands) + k: k for k in range(len(saved))},
                compiler_params=params(58),
                cost_estimate=cost(3 * mat, 10e6),
                name="attention_forward",
            )(*operands, *saved)
            if ring and n == 0:
                chain.last = mark
                later.over_corner()
            elif ring:
                chain.last = mark
                near2, far2 = later.over_core()
        query, keys, values, attended, probs = saved

        lanes = rows_of((block, 128))
        ff_rows = rows_of((block, ff))
        feed_scratch = [pltpu.VMEM((width, ff // 2), bf16), pltpu.VMEM((ff // 2, width), bf16)]
        weights = (own_o, own_i, own_u, near2, far2)
        (
            xhat1, s1, h1, active, slope, xhat2, s2, acts, pooled, payload
        ) = pl.pallas_call(
            feed_forward(seq, width),
            grid=(steps,),
            in_specs=[SCALARS, SCALARS, SCALARS, wide_rows, wide_rows]
            + [whole(v.shape) for v in (vec, bias) + weights],
            out_specs=[
                wide_rows, lanes, wide_rows, ff_rows, ff_rows, wide_rows, lanes, wide_rows,
                whole((sentences, width)), whole((sentences, width + 128)),
            ],
            out_shape=[
                arr(width, f32), arr(128, f32), arr(width, bf16), arr(ff, bf16), arr(ff, bf16),
                arr(width, f32), arr(128, f32), arr(width, bf16), arr(width, f32, sentences),
                arr(width + 128, f32, sentences),
            ],
            scratch_shapes=[square] + feed_scratch,
            compiler_params=params(56),
            cost_estimate=cost(9 * mat, 40e6),
            name="feed_forward",
        )(lens, place, pair_language, flat, attended, vec, bias, *weights)

        gathered = gather_units(payload, n_dp, n_fs, ring)
        lens_units = lengths.T.reshape(sentences).astype(f32)
        devices = n_dp * n_fs
        if devices * pairs <= 512:
            dpool = pl.pallas_call(
                loss_kernel,
                in_specs=[FULL] * 3,
                out_specs=FULL,
                out_shape=arr(width, f32, sentences),
                cost_estimate=cost(2e9, 2e6),
                compiler_params=pltpu.CompilerParams(vmem_limit_bytes=32 * 1024 * 1024),
                name="pair_loss",
            )(gathered, pooled, jnp.broadcast_to(lens_units[:, None], (sentences, 128)))
        else:
            sides = gathered.reshape(devices, 2, pairs, width + 128)
            lang = sides[:, 0, :, width].reshape(-1)
            dpool = pool_grad(
                sides[:, 0, :, :width].reshape(-1, width),
                sides[:, 1, :, :width].reshape(-1, width),
                lang[:, None], lang[None, :], pooled, lens_units[:, None], pairs,
            )

        dy, dz, dr1, do, sums, inner_sums = pl.pallas_call(
            feed_backward(seq, width),
            grid=(steps,),
            in_specs=[SCALARS, SCALARS, whole(dpool.shape), whole(vec.shape), wide_rows, lanes,
                      ff_rows, wide_rows, lanes]
            + [whole(v.shape) for v in weights],
            out_specs=[wide_rows, ff_rows, wide_rows, wide_rows, whole((8, width)), whole((8, ff))],
            out_shape=[arr(width, bf16), arr(ff, bf16), arr(width, f32), arr(width, bf16),
                       arr(width, f32, 8), arr(ff, f32, 8)],
            scratch_shapes=feed_scratch,
            compiler_params=params(56),
            cost_estimate=cost(8 * mat, 40e6),
            name="feed_backward",
        )(lens, place, dpool, vec, xhat2, s2, slope, xhat1, s1, *weights)

        outer_grad = mm_rows(active, dy).astype(bf16)
        inner_grad = mm_rows(h1, dz).astype(bf16)
        o_grad = mm_rows(attended, do).astype(bf16)
        ff_own = own_u.shape[0]
        q_rows = half // 2

        def square_lines(grads, is_own, c):
            h = f if is_own else 1 - f
            return [cut(g, h * half + c * q_rows, q_rows) for g in grads]

        def stacked(make):
            return lambda c: jnp.stack(
                [jnp.concatenate(make(is_own, c), axis=0) for is_own in (True, False)]
            )

        def outer_lines(is_own, c):
            base = 0 if is_own else ff_own
            return [cut(outer_grad[base : base + ff_own], c * (ff_own // 2), ff_own // 2)]

        def inner_lines(is_own, c):
            base = 0 if is_own else ff_own
            lines = cut(inner_grad, c * half, half)[:, base : base + ff_own]
            return [lines[:, s : s + width] for s in range(0, ff_own, width)] + square_lines(
                (o_grad,), is_own, c
            )

        gate = dr1
        if ring:
            chain = Chain()
            outer_red = Reducer(stacked(outer_lines), chain, n_dp, n_fs, dp_index)
            inner_red = Reducer(stacked(inner_lines), chain, n_dp, n_fs, dp_index)
            outer_red.x()
            inner_red.y()
            gate, _ = lax.optimization_barrier((dr1, chain.last))
        back, sums_parts = (), []
        for n in range(parts):
            if n == 1 and ring:
                chain.last = part_sums
                outer_red.y()
                gate, _ = lax.optimization_barrier((gate, chain.last))
            operands = (
                place, gate, query, keys, values, probs, own_q, own_k, own_v, near, far, own_o,
                near2, far2,
            )
            *back, part_sums = pl.pallas_call(
                attention_backward(seq, factor, len(back)),
                grid=(fewer,),
                in_specs=[SCALARS] + [offset_rows(width, n)] * 5
                + [whole(v.shape) for v in operands[6:]] + [any_space] * len(back),
                out_specs=[offset_rows(width, n)] * 4 + [whole((8, width))],
                out_shape=[arr(width, f32)] + [arr(width, bf16)] * 3 + [arr(width, f32, 8)],
                scratch_shapes=[square] * 4 + [pltpu.VMEM((block, width), bf16)],
                input_output_aliases={len(operands) + k: k for k in range(len(back))},
                compiler_params=params(58),
                cost_estimate=cost(5 * mat, 15e6),
                name="attention_backward",
            )(*operands, *back)
            sums_parts.append(part_sums)
        din, dq, dk, dv = back
        attn_sums = sum(sums_parts[1:], sums_parts[0])

        q_grad, k_grad, v_grad = [mm_rows(flat, d).astype(bf16) for d in (dq, dk, dv)]
        vec_grad = jnp.concatenate([attn_sums[0:2], sums[0:6]], axis=0)
        bias_grad = inner_sums[0]
        acts = acts.reshape(tokens.shape)
        din = din.reshape(tokens.shape)

        if not ring:
            def settle(value, axis=0):
                low = lax.psum_scatter(
                    value.astype(bf16), "fsdp", scatter_dimension=axis, tiled=True
                )
                return lax.psum(low.astype(f32), "dp")

            vec_out = settle(vec_grad, 1)
            squares = [settle(g) for g in (q_grad, k_grad, v_grad, o_grad)]
            inner_out, outer_out = settle(inner_grad, 1), settle(outer_grad)
            bias_out = settle(bias_grad)
        else:
            vec_half = vec_grad.reshape(len(small), 2, half).transpose(1, 0, 2)
            vec_half = vec_half.reshape(2, -1, width)
            bias_half = bias_grad.reshape(2, -1, width)
            vec_rows, bias_rows = vec_half.shape[1], bias_half.shape[1]
            tail = 64 - vec_rows - bias_rows

            def late_lines(is_own, c):
                h = f if is_own else 1 - f
                extra = jnp.concatenate(
                    [
                        lax.dynamic_index_in_dim(vec_half, h, 0, keepdims=False),
                        bias_half[0 if is_own else 1],
                        jnp.zeros((tail, width), f32),
                    ],
                    axis=0,
                )
                extra = jnp.where(c == 0, extra, 0.0).astype(bf16)
                return square_lines((v_grad,), is_own, c) + [extra]

            def early_lines(is_own, c):
                return square_lines((q_grad, k_grad), is_own, c)

            chain.last = part_sums
            inner_red.x()
            outer_red.z()
            pair_red = Reducer(stacked(early_lines), chain, n_dp, n_fs, dp_index)
            last_red = Reducer(stacked(late_lines), chain, n_dp, n_fs, dp_index)
            pair_red.x()
            last_red.y()
            outer_red.back_z()
            inner_red.z()
            last_red.x()
            pair_red.y()
            outer_red.back_y()
            last_red.z()
            pair_red.z()
            inner_red.back_z()
            outer_red.back_core()
            last_red.back_z()
            pair_red.back_z()
            inner_red.back_y()
            last_red.back_y()
            pair_red.back_y()
            inner_red.back_core()
            last_red.back_core()
            pair_red.back_core()
            (outer0, outer1), (inner0, inner1), (pair0, pair1), (last0, last1) = [
                r.halves for r in (outer_red, inner_red, pair_red, last_red)
            ]
            outer_out = jnp.concatenate([outer0, outer1], axis=0).astype(f32)
            cuts = ff_own // width * half
            inner_out = jnp.concatenate(
                [
                    jnp.concatenate([p[s : s + half] for s in range(0, cuts, half)], axis=1)
                    for p in (inner0, inner1)
                ],
                axis=0,
            ).astype(f32)

            def square_out(first, second, start):
                return jnp.concatenate(
                    [p[start : start + q_rows] for p in (first, second)], axis=0
                ).astype(f32)

            squares = [
                square_out(pair0, pair1, 0),
                square_out(pair0, pair1, q_rows),
                square_out(last0, last1, 0),
                square_out(inner0, inner1, cuts),
            ]
            extra = last0[q_rows:]
            vec_out = extra[:vec_rows].reshape(len(small), half).astype(f32)
            bias_out = extra[vec_rows : vec_rows + bias_rows].reshape(-1).astype(f32)

        return (
            acts, din, squares[0], squares[1], squares[2], squares[3],
            vec_out[0], vec_out[1], vec_out[2], vec_out[3], vec_out[4],
            inner_out, bias_out, outer_out, vec_out[5], vec_out[6], vec_out[7],
        )

    return body


def solution(mesh):
    both = ("dp", "fsdp")
    vector, matrix = P("fsdp"), P("fsdp", None)
    in_specs = (
        (P(both, None, None, None), P(both, None), P(both))
        + (matrix,) * 4
        + (vector,) * 5
        + (P(None, "fsdp"), vector, matrix, vector, vector, vector)
    )
    out_specs = (
        (P(both, None, None, None),) * 2
        + (matrix,) * 4
        + (vector,) * 5
        + (P(None, "fsdp"), vector, matrix, vector, vector, vector)
    )
    return jax.shard_map(
        step_body(mesh.shape["dp"], mesh.shape["fsdp"]),
        mesh=mesh,
        in_specs=in_specs,
        out_specs=out_specs,
        check_vma=False,
    )
```
